32 devices in a mesh: vel: 16 (over z, x, core), gx: 2 (over y).
Axes of the slice: x: 2, y: 2, z: 4, core: 2. Of those that a mesh axis runs over, the one named last changes fastest.
Arguments:
- distribution: float32 [4096, 8, 256], P('vel', 'gx'), as said below
Outputs:
- relaxed: float32 [4096, 8, 256], P('vel', 'gx')
Inputs may be any that keep to these rules, and one draw needn't show every extreme that they name: `distribution`: every entry is positive.
All inputs are finite; a program needn't handle non-finite values.
Results may differ from the reference program's by a relative error of at most 0.0003.
Values sent between devices are 32-bit elements; how exact they have to be, the bound alone decides.
A program may use at most 64 MiB of HBM per device.

```python
import math
import jax
import jax.numpy as jnp
from jax import lax

NV1 = 16
V = 4096
NY = 16
NZ = 16
COLLISIONS = 2
NX = 8


def draw_distribution(key, part):
    keys = jax.random.split(jax.random.fold_in(key, 17), 4)
    cells = NX * NY * NZ
    rho = jnp.exp(jax.random.uniform(keys[0], (cells,), jnp.float32, math.log(0.5), math.log(2.0)))
    drift = jax.random.uniform(keys[1], (3, cells), jnp.float32, -1.0, 1.0)
    temp = jnp.exp(jax.random.uniform(keys[2], (cells,), jnp.float32, math.log(0.6), math.log(2.5)))
    rough = 0.4 * jax.random.uniform(keys[3], (V, cells), jnp.float32, -1.0, 1.0)
    spacing = 8.0 / (NV1 - 1)
    index = jnp.arange(V, dtype=jnp.int32)
    first = (-4.0 + spacing * (index % NV1).astype(jnp.float32))[:, None]
    second = (-4.0 + spacing * (index // NV1 // NV1).astype(jnp.float32))[:, None]
    third = (-4.0 + spacing * (index // NV1 % NV1).astype(jnp.float32))[:, None]
    spread = (first - drift[0]) ** 2 + (second - drift[1]) ** 2 + (third - drift[2]) ** 2
    field = rho * temp ** (-1.5) * jnp.exp(-spread / (2.0 * temp)) * (1.0 + rough)
    return field.reshape(V, NX, NY * NZ).astype(jnp.float32)


def setup_inputs(seed: int = 0) -> dict:
    key_of = jax.random.split(jax.random.key(seed), 2)
    distribution = draw_distribution(jax.random.fold_in(key_of[1], 71), 0)
    return {"distribution": distribution}


speed_limit = 4.0
time_step = 0.05
knudsen = 0.0125
vel_block = 256

def velocities(index):
    spacing = 2.0 * speed_limit / (NV1 - 1)
    first = index % NV1
    rest = index // NV1
    second = rest // NV1
    third = rest % NV1
    return [-speed_limit + spacing * part.astype(jnp.float32) for part in (first, second, third)]

def quad_weight():
    spacing = 2.0 * speed_limit / (NV1 - 1)
    return spacing ** 3 / (2.0 * math.pi) ** 1.5

def along_z(field, offset):
    zpos = jnp.arange(field.shape[-1], dtype=jnp.int32) % NZ
    main = jnp.roll(field, offset, -1)
    if offset > 0:
        other = jnp.roll(field, offset - NZ, -1)
        keep = zpos >= offset
    else:
        other = jnp.roll(field, offset + NZ, -1)
        keep = zpos < NZ + offset
    return jnp.where(keep, main, other)

def backward(field, minus_one, minus_two):
    return (3.0 * field - 4.0 * minus_one + minus_two) * 0.5

def forward(field, plus_one, plus_two):
    return (-3.0 * field + 4.0 * plus_one - plus_two) * 0.5

def upwind(field, comp, minus_one, minus_two, plus_one, plus_two):
    return jnp.where(comp > 0, backward(field, minus_one, minus_two), forward(field, plus_one, plus_two))

def transverse(field, comp_y, comp_z):
    deriv_y = upwind(field, comp_y, jnp.roll(field, NZ, -1), jnp.roll(field, 2 * NZ, -1), jnp.roll(field, -NZ, -1), jnp.roll(field, -2 * NZ, -1))
    deriv_z = upwind(field, comp_z, along_z(field, 1), along_z(field, 2), along_z(field, -1), along_z(field, -2))
    return (deriv_y, deriv_z)

def rate(field, comp_x, comp_y, comp_z):
    deriv_x = upwind(field, comp_x, jnp.roll(field, 1, 1), jnp.roll(field, 2, 1), jnp.roll(field, -1, 1), jnp.roll(field, -2, 1))
    deriv_y, deriv_z = transverse(field, comp_y, comp_z)
    return -(comp_x * deriv_x + comp_y * deriv_y + comp_z * deriv_z)

def advance(field, comp_x, comp_y, comp_z):
    first = field + time_step * rate(field, comp_x, comp_y, comp_z)
    second = 0.75 * field + 0.25 * (first + time_step * rate(first, comp_x, comp_y, comp_z))
    return field / 3.0 + 2.0 / 3.0 * (second + time_step * rate(second, comp_x, comp_y, comp_z))

def primitive(moments):
    rho = moments[0]
    vel_x = moments[1] / rho
    vel_y = moments[2] / rho
    vel_z = moments[3] / rho
    temp = (moments[4] / rho - (vel_x * vel_x + vel_y * vel_y + vel_z * vel_z)) / 3.0
    return jnp.stack([rho, vel_x, vel_y, vel_z, temp])

def maxwell(prims, comp_x, comp_y, comp_z):
    spread = (comp_x - prims[1]) ** 2 + (comp_y - prims[2]) ** 2 + (comp_z - prims[3]) ** 2
    return prims[0] * prims[4] ** (-1.5) * jnp.exp(-spread / (2.0 * prims[4]))

def moment_table(comp_x, comp_y, comp_z):
    ones = jnp.ones_like(comp_x)
    return jnp.stack([ones, comp_x, comp_y, comp_z, comp_x * comp_x + comp_y * comp_y + comp_z * comp_z]) * quad_weight()

def reference(distribution):
    blocks = V // vel_block
    index = jnp.arange(V, dtype=jnp.int32)
    comp = jnp.stack(velocities(index), 1).reshape(blocks, vel_block, 3)
    field = distribution.reshape(blocks, vel_block, NX, NY * NZ)

    def stream(args):
        block, cv = args
        return advance(block, cv[:, 0][:, None, None], cv[:, 1][:, None, None], cv[:, 2][:, None, None])
    for step in range(COLLISIONS):
        field = lax.map(stream, (field, comp))

        def moment_block(args):
            block, cv = args
            table = moment_table(cv[:, 0], cv[:, 1], cv[:, 2])
            return jnp.dot(table, block.reshape(vel_block, -1), precision=lax.Precision.HIGHEST)
        moments = lax.optimization_barrier(jnp.sum(lax.map(moment_block, (field, comp)), 0))
        prims = primitive(moments)

        def mass_block(cv):
            local = maxwell(prims, cv[:, 0][:, None], cv[:, 1][:, None], cv[:, 2][:, None])
            return quad_weight() * lax.optimization_barrier(jnp.sum(local, 0))
        mass = lax.optimization_barrier(jnp.sum(lax.map(mass_block, comp), 0))
        scale = prims[0] / mass
        rates = time_step * prims[0] * jnp.sqrt(prims[4]) / knudsen

        def relax(args):
            block, cv = args
            local = maxwell(prims, cv[:, 0][:, None], cv[:, 1][:, None], cv[:, 2][:, None])
            flat = block.reshape(vel_block, -1)
            return ((flat + rates * (local * scale)) / (1.0 + rates)).reshape(block.shape)
        field = lax.map(relax, (field, comp))
    return field.reshape(V, NX, NY * NZ)
```

```python
import functools
import math

import jax
import jax.numpy as jnp
from jax import lax
from jax.experimental import pallas as pl
from jax.experimental.pallas import tpu as pltpu
from jax.sharding import PartitionSpec as P

NV1 = 16
NZ = 16
COLLISIONS = 2
MOMENTS = 5
BLOCK = 4
MESH = pl.DeviceIdType.MESH

speed_limit = 4.0
time_step = 0.05
knudsen = 0.0125
spacing = 2.0 * speed_limit / (NV1 - 1)
weight = spacing**3 / (2.0 * math.pi) ** 1.5


def loop(count, body):
    def wrapped(i, carry):
        body(i)
        return carry

    lax.fori_loop(0, count, wrapped, 0)


def component(index):
    return -speed_limit + spacing * index.astype(jnp.float32)


def streamed(field, cx0, cy, cz):
    shape = field.shape
    nx, cells = shape[1], shape[2]
    ahead = (cx0 > 0, cy > 0, cz > 0)
    sx1 = jnp.where(ahead[0], 1, nx - 1)
    sx2 = jnp.where(ahead[0], 2, nx - 2)
    sy1 = jnp.where(ahead[1], NZ, cells - NZ)
    sy2 = jnp.where(ahead[1], 2 * NZ, cells - 2 * NZ)
    sz1 = jnp.where(ahead[2], 1, cells - 1)
    sz2 = jnp.where(ahead[2], 2, cells - 2)
    wz1 = jnp.where(ahead[2], cells + 1 - NZ, NZ - 1)
    wz2 = jnp.where(ahead[2], cells + 2 - NZ, NZ - 2)
    zpos = lax.broadcasted_iota(jnp.int32, shape, 2) % NZ
    depth = jnp.where(ahead[2], 0, NZ - 1) + jnp.where(ahead[2], 1, -1) * zpos
    keep1, keep2 = depth >= 1, depth >= 2
    half = 0.5 * time_step
    step = lax.broadcasted_iota(jnp.int32, shape, 0).astype(jnp.float32)
    kx = half * jnp.abs(cx0 + spacing * step)
    ky = half * jnp.abs(cy)
    kz = half * jnp.abs(cz)
    centre = 3.0 * (kx + (ky + kz))

    def change(g):
        x1, x2 = pltpu.roll(g, sx1, 1), pltpu.roll(g, sx2, 1)
        y1, y2 = pltpu.roll(g, sy1, 2), pltpu.roll(g, sy2, 2)
        z1 = jnp.where(keep1, pltpu.roll(g, sz1, 2), pltpu.roll(g, wz1, 2))
        z2 = jnp.where(keep2, pltpu.roll(g, sz2, 2), pltpu.roll(g, wz2, 2))
        gain = kx * (4.0 * x1 - x2) + ky * (4.0 * y1 - y2) + kz * (4.0 * z1 - z2)
        return gain - centre * g

    first = field + change(field)
    second = 0.75 * field + 0.25 * (first + change(first))
    return field * (1.0 / 3.0) + (2.0 / 3.0) * (second + change(second))


def fill_tables(moments, table, factor):
    rho = moments[0]
    ux, uy, uz = moments[1] / rho, moments[2] / rho, moments[3] / rho
    temp = (moments[4] / rho - (ux * ux + uy * uy + uz * uz)) / 3.0
    inverse = -0.5 / temp
    mass = None
    for d, u in enumerate((ux, uy, uz)):
        total = None
        for i in range(NV1):
            offset = (-speed_limit + spacing * i) - u
            value = jnp.exp(offset * offset * inverse)
            table[d, i] = value
            total = value if total is None else total + value
        mass = total if mass is None else mass * total
    nu = time_step * rho * jnp.sqrt(temp) / knudsen
    keep = 1.0 / (1.0 + nu)
    factor[0] = keep
    factor[1] = keep * nu * (rho / (weight * mass))


def kernel(
    nv, ng, src, out, slab, field, back, part, inbox, total, table, factor, table2, factor2,
    own_sem, in_send, in_recv, out_send, out_recv, rs_send, rs_recv, ag_send, ag_recv,
):
    count, xs, cells = src.shape
    n = count // ng
    nx = ng * xs
    nc = in_send.shape[1]
    size = n // nc
    ranks = nv * ng
    v, g = lax.axis_index("vel"), lax.axis_index("gx")
    me = v * ng + g

    barrier = pltpu.get_barrier_semaphore()

    def greet(i):
        other = lax.rem(me + i + 1, ranks)
        pl.semaphore_signal(barrier, 1, device_id=(other // ng, lax.rem(other, ng)), device_id_type=MESH)

    loop(ranks - 1, greet)
    own = pltpu.make_async_copy(src.at[pl.ds(g * n, n)], slab.at[g], own_sem)
    own.start()
    pl.semaphore_wait(barrier, ranks - 1)

    def incoming(d, c):
        to = lax.rem(g + d, ng)
        return pltpu.make_async_remote_copy(
            src_ref=src.at[pl.ds(to * n + c * size, size)],
            dst_ref=slab.at[g, pl.ds(c * size, size)],
            send_sem=in_send.at[d - 1, c],
            recv_sem=in_recv.at[d - 1, c],
            device_id=(v, to),
            device_id_type=MESH,
        )

    def outgoing(d, c):
        to = lax.rem(g + d, ng)
        return pltpu.make_async_remote_copy(
            src_ref=slab.at[to, pl.ds(c * size, size)],
            dst_ref=back.at[g, pl.ds(c * size, size)],
            send_sem=out_send.at[d - 1, c],
            recv_sem=out_recv.at[d - 1, c],
            device_id=(v, to),
            device_id_type=MESH,
        )

    def each(make, act, first=0, last=nc):
        def over(c):
            for d in range(1, ng):
                act(make(d, c + first))

        loop(last - first, over)

    each(incoming, lambda copy: copy.start())
    own.wait()

    def parts_of(k):
        ix = lax.rem(k, NV1)
        iz = lax.rem(k // NV1, NV1)
        iy = k // (NV1 * NV1)
        return ix, iy, iz

    def velocity_block(j, load, store, sums):
        ix, iy, iz = parts_of(v * count + g * n + j)
        cx0, cy, cz = component(ix), component(iy), component(iz)
        read = streamed(load(j, ix, iy, iz), cx0, cy, cz)
        store(j, read)
        s0 = s1 = s2 = None
        for b in range(BLOCK):
            cx = cx0 + spacing * b
            one = read[b]
            m1 = cx * one
            m2 = cx * m1
            s0 = one if s0 is None else s0 + one
            s1 = m1 if s1 is None else s1 + m1
            s2 = m2 if s2 is None else s2 + m2
        return (
            sums[0] + s0,
            sums[1] + s1,
            sums[2] + cy * s0,
            sums[3] + cz * s0,
            sums[4] + (s2 + (cy * cy + cz * cz) * s0),
        )

    def chunk(c, load, store, sums):
        def body(i, carry):
            return velocity_block(c * size + i * BLOCK, load, store, carry)

        return lax.fori_loop(0, size // BLOCK, body, sums)

    zero = tuple(jnp.zeros((nx, cells), jnp.float32) for _ in range(MOMENTS))
    owner = [(i * nv) // MOMENTS for i in range(MOMENTS)]
    is_owner = functools.reduce(jnp.logical_or, [v == o for o in owner])

    def write_part(which, sums):
        for i in range(MOMENTS):
            for s in range(ng):
                part[which, i, s] = weight * sums[i][s * xs : (s + 1) * xs]

    def scatter(which):
        for i, o in enumerate(owner):
            def over(s, i=i, o=o):
                @pl.when(jnp.logical_not(jnp.logical_and(v == o, g == s)))
                def _():
                    slot = lax.rem(me - (o * ng + s) - 1 + ranks, ranks)
                    pltpu.make_async_remote_copy(
                        src_ref=part.at[which, i, s],
                        dst_ref=inbox.at[which, slot],
                        send_sem=rs_send.at[which],
                        recv_sem=rs_recv.at[which],
                        device_id=(o, s),
                        device_id_type=MESH,
                    ).start()

            loop(ng, over)

    def local(ref, sem):
        return pltpu.make_async_copy(ref, ref, sem)

    def gather(which, everyone):
        peers = ranks if everyone else nv
        for i, o in enumerate(owner):
            @pl.when(v == o)
            def _(i=i):
                local(inbox.at[which], rs_recv.at[which]).wait()

                def add(k, acc):
                    return acc + inbox[which, k]

                acc = lax.fori_loop(0, ranks - 1, add, part[which, i, g])
                total[which, i * ng + g] = acc

                def send(k):
                    if everyone:
                        other = lax.rem(me + k + 1, ranks)
                        target = (other // ng, lax.rem(other, ng))
                    else:
                        target = (lax.rem(v + k + 1, nv), g)
                    pltpu.make_async_remote_copy(
                        src_ref=total.at[which, i * ng + g],
                        dst_ref=total.at[which, i * ng + g],
                        send_sem=ag_send.at[which],
                        recv_sem=ag_recv.at[which],
                        device_id=target,
                        device_id_type=MESH,
                    ).start()

                loop(peers - 1, send)

        items = MOMENTS * ng if everyone else MOMENTS

        @pl.when(is_owner)
        def _():
            local(total.at[which, pl.ds(0, items - 1)], ag_recv.at[which]).wait()

        @pl.when(jnp.logical_not(is_owner))
        def _():
            local(total.at[which, pl.ds(0, items)], ag_recv.at[which]).wait()

    def drain(which, everyone):
        peers = ranks if everyone else nv

        items = MOMENTS * ng

        @pl.when(is_owner)
        def _():
            local(total.at[which, pl.ds(0, items - 1)], rs_send.at[which]).wait()
            local(inbox.at[which, pl.ds(0, peers - 1)], ag_send.at[which]).wait()

        @pl.when(jnp.logical_not(is_owner))
        def _():
            local(total.at[which], rs_send.at[which]).wait()

    def load_first(j, ix, iy, iz):
        return jnp.concatenate([slab[s, pl.ds(j, BLOCK)] for s in range(ng)], axis=1)

    def store_first(j, read):
        field[pl.ds(j, BLOCK)] = read

    def first_chunk(c, sums):
        for d in range(1, ng):
            incoming(d, c).wait_recv()
        return chunk(c, load_first, store_first, sums)

    sums = lax.fori_loop(0, nc, first_chunk, zero)
    write_part(0, sums)
    scatter(0)
    each(incoming, lambda copy: copy.wait_send())
    gather(0, True)
    fill_tables(
        [jnp.concatenate([total[0, i * ng + s] for s in range(ng)], axis=0) for i in range(MOMENTS)],
        table,
        factor,
    )

    def load_second(j, ix, iy, iz):
        rest = factor[1] * table[1, iy] * table[2, iz]
        return factor[0] * field[pl.ds(j, BLOCK)] + rest * table[0, pl.ds(ix, BLOCK)]

    def store_second(j, read):
        for s in range(ng):
            slab[s, pl.ds(j, BLOCK)] = read[:, s * xs : (s + 1) * xs]

    early = nc // 2

    def second_chunk(c, sums):
        return chunk(c, load_second, store_second, sums)

    def second_sent(c, sums):
        sums = second_chunk(c, sums)
        for d in range(1, ng):
            outgoing(d, c).start()
        return sums

    sums = lax.fori_loop(0, early, second_sent, zero)
    sums = lax.fori_loop(early, nc, second_chunk, sums)
    write_part(1, sums)
    scatter(1)
    each(outgoing, lambda copy: copy.start(), early, nc)
    drain(0, True)
    gather(1, False)
    fill_tables([total[1, i * ng + g] for i in range(MOMENTS)], table2, factor2)

    def relax(source, s, c):
        def body(i):
            j = c * size + i * BLOCK
            ix, iy, iz = parts_of(v * count + s * n + j)
            rest = factor2[1] * table2[1, iy] * table2[2, iz]
            out[pl.ds(s * n + j, BLOCK)] = (
                factor2[0] * source[s, pl.ds(j, BLOCK)] + rest * table2[0, pl.ds(ix, BLOCK)]
            )

        loop(size // BLOCK, body)

    loop(nc, lambda c: relax(slab, g, c))

    def last(c):
        for d in range(1, ng):
            outgoing(d, c).wait_recv()
            relax(back, lax.rem(g - d + ng, ng), c)

    loop(nc, last)
    each(outgoing, lambda copy: copy.wait_send())
    drain(1, False)


def on_device(distribution):
    nv, ng = lax.axis_size("vel"), lax.axis_size("gx")
    count, xs, cells = distribution.shape
    n = count // ng
    nx = xs * ng
    size = max(BLOCK, n // 8)
    nc = n // size
    f32 = jnp.float32
    dma = pltpu.SemaphoreType.DMA
    return pl.pallas_call(
        functools.partial(kernel, nv, ng),
        out_shape=jax.ShapeDtypeStruct(distribution.shape, f32),
        in_specs=[pl.BlockSpec(memory_space=pl.ANY)],
        out_specs=pl.BlockSpec(memory_space=pltpu.VMEM),
        scratch_shapes=[
            pltpu.VMEM((ng, n, xs, cells), f32),
            pltpu.VMEM((n, nx, cells), f32),
            pltpu.VMEM((ng, n, xs, cells), f32),
            pltpu.VMEM((COLLISIONS, MOMENTS, ng, xs, cells), f32),
            pltpu.VMEM((COLLISIONS, nv * ng - 1, xs, cells), f32),
            pltpu.VMEM((COLLISIONS, MOMENTS * ng, xs, cells), f32),
            pltpu.VMEM((3, NV1, nx, cells), f32),
            pltpu.VMEM((2, nx, cells), f32),
            pltpu.VMEM((3, NV1, xs, cells), f32),
            pltpu.VMEM((2, xs, cells), f32),
            dma(()),
            dma((max(ng - 1, 1), nc)),
            dma((max(ng - 1, 1), nc)),
            dma((max(ng - 1, 1), nc)),
            dma((max(ng - 1, 1), nc)),
            dma((COLLISIONS,)),
            dma((COLLISIONS,)),
            dma((COLLISIONS,)),
            dma((COLLISIONS,)),
        ],
        compiler_params=pltpu.CompilerParams(collective_id=0, has_side_effects=True),
    )(distribution)


def solution(mesh):
    return jax.shard_map(
        on_device,
        mesh=mesh,
        in_specs=(P("vel", "gx", None),),
        out_specs=P("vel", "gx", None),
        check_vma=False,
    )
```

```python
import functools
import math

import jax
import jax.numpy as jnp
from jax import lax
from jax.experimental import pallas as pl
from jax.experimental.pallas import tpu as pltpu
from jax.sharding import PartitionSpec as P

NV1 = 16
NZ = 16
COLLISIONS = 2
MOMENTS = 5
BLOCK = 4
LANES = 128
MESH = pl.DeviceIdType.MESH

speed_limit = 4.0
time_step = 0.05
knudsen = 0.0125
spacing = 2.0 * speed_limit / (NV1 - 1)
weight = spacing**3 / (2.0 * math.pi) ** 1.5


def loop(count, body):
    def wrapped(i, carry):
        body(i)
        return carry

    lax.fori_loop(0, count, wrapped, 0)


def component(index):
    return -speed_limit + spacing * index.astype(jnp.float32)


def streamed(field, ix0, cy, cz):
    shape = field.shape
    nx, cells = shape[1], shape[2]
    lanes = min(LANES, cells)
    pieces = cells // lanes
    fields = [field[:, :, h * lanes : (h + 1) * lanes] for h in range(pieces)]
    shape = fields[0].shape
    up_x = ix0 >= NV1 // 2
    up_y, up_z = cy > 0, cz > 0
    lane = lax.broadcasted_iota(jnp.int32, shape, 2)
    zpos = lane % NZ
    depth_z = jnp.where(up_z, 0, NZ - 1) + jnp.where(up_z, 1, -1) * zpos
    depth_y = jnp.where(up_y, 0, lanes - 1) + jnp.where(up_y, 1, -1) * lane
    half = 0.5 * time_step
    speeds = [abs(-speed_limit + spacing * (ix0 + b)) for b in range(shape[0])]
    ay, az = jnp.abs(cy), jnp.abs(cz)
    amount_y = [jnp.where(up_y, k * NZ, lanes - k * NZ) for k in (1, 2)]
    amount_z = [jnp.where(up_z, k, lanes - k) for k in (1, 2)]
    wrap_z = [jnp.where(up_z, lanes + k - NZ, NZ - k) for k in (1, 2)]
    keep_y = [depth_y >= k * NZ for k in (1, 2)]
    keep_z = [depth_z >= k for k in (1, 2)]

    def advanced(gs, factor):
        scale = factor * half
        ky, kz = scale * ay, scale * az
        kx = [scale * speed for speed in speeds]
        centre = [3.0 * (k + (ky + kz)) for k in kx]
        spread = lambda values: jnp.stack([jnp.full(shape[1:], k, jnp.float32) for k in values])
        kx, centre = spread(kx), spread(centre)
        fours = [4.0 * g for g in gs]
        y1 = [pltpu.roll(g, amount_y[0], 2) for g in fours]
        y2 = [pltpu.roll(g, amount_y[1], 2) for g in gs]

        def across(turned, h, keep):
            if pieces == 1:
                return turned[h]
            if pieces == 2:
                return jnp.where(keep, turned[h], turned[1 - h])
            other = jnp.where(up_y, turned[h - 1], turned[(h + 1) % pieces])
            return jnp.where(keep, turned[h], other)

        result = []
        for h, (f, g, four) in enumerate(zip(fields, gs, fours)):
            dx = pltpu.roll(four, 1 if up_x else nx - 1, 1) - pltpu.roll(g, 2 if up_x else nx - 2, 1)
            dy = across(y1, h, keep_y[0]) - across(y2, h, keep_y[1])
            z1 = jnp.where(keep_z[0], pltpu.roll(four, amount_z[0], 2), pltpu.roll(four, wrap_z[0], 2))
            z2 = jnp.where(keep_z[1], pltpu.roll(g, amount_z[1], 2), pltpu.roll(g, wrap_z[1], 2))
            result.append((f - centre * g) + kx * dx + ky * dy + kz * (z1 - z2))
        return result

    value = advanced(fields, 1.0 / 3.0)
    value = advanced(value, 0.5)
    return advanced(value, 1.0)


def fill_tables(moments, table, factor):
    rho = moments[0]
    ux, uy, uz = moments[1] / rho, moments[2] / rho, moments[3] / rho
    temp = (moments[4] / rho - (ux * ux + uy * uy + uz * uz)) / 3.0
    inverse = -0.5 / temp
    mass = None
    for d, u in enumerate((ux, uy, uz)):
        total = None
        for i in range(NV1):
            offset = (-speed_limit + spacing * i) - u
            value = jnp.exp(offset * offset * inverse)
            table[d, i] = value
            total = value if total is None else total + value
        mass = total if mass is None else mass * total
    nu = time_step * rho * jnp.sqrt(temp) / knudsen
    keep = 1.0 / (1.0 + nu)
    factor[0] = keep
    factor[1] = keep * nu * (rho / (weight * mass))


def kernel(
    nv, ng, src, out, slab, field, back, part, inbox, total, table, factor, table2, factor2,
    own_sem, in_send, in_recv, out_send, out_recv, rs_send, rs_recv, ag_send, ag_recv,
):
    count, xs, cells = src.shape
    n = count // ng
    nx = ng * xs
    nc = in_send.shape[1]
    size = n // nc
    ranks = nv * ng
    v, g = lax.axis_index("vel"), lax.axis_index("gx")
    me = v * ng + g

    barrier = pltpu.get_barrier_semaphore()

    def greet(i):
        other = lax.rem(me + i + 1, ranks)
        pl.semaphore_signal(barrier, 1, device_id=(other // ng, lax.rem(other, ng)), device_id_type=MESH)

    loop(ranks - 1, greet)
    own = pltpu.make_async_copy(src.at[pl.ds(g * n, n)], slab.at[g], own_sem)
    own.start()
    pl.semaphore_wait(barrier, ranks - 1)

    def incoming(d, c):
        to = lax.rem(g + d, ng)
        return pltpu.make_async_remote_copy(
            src_ref=src.at[pl.ds(to * n + c * size, size)],
            dst_ref=slab.at[g, pl.ds(c * size, size)],
            send_sem=in_send.at[d - 1, c],
            recv_sem=in_recv.at[d - 1, c],
            device_id=(v, to),
            device_id_type=MESH,
        )

    def outgoing(d, c):
        to = lax.rem(g + d, ng)
        return pltpu.make_async_remote_copy(
            src_ref=slab.at[to, pl.ds(c * size, size)],
            dst_ref=back.at[g, pl.ds(c * size, size)],
            send_sem=out_send.at[d - 1, c],
            recv_sem=out_recv.at[d - 1, c],
            device_id=(v, to),
            device_id_type=MESH,
        )

    def each(make, act, first=0, last=nc):
        def over(c):
            for d in range(1, ng):
                act(make(d, c + first))

        loop(last - first, over)

    each(incoming, lambda copy: copy.start())
    own.wait()

    def parts_of(k):
        ix = lax.rem(k, NV1)
        iz = lax.rem(k // NV1, NV1)
        iy = k // (NV1 * NV1)
        return ix, iy, iz

    def velocity_row(j, load, store, sums):
        _, iy, iz = parts_of(v * count + g * n + j)
        cy, cz = component(iy), component(iz)
        rest = load.prepare(iy, iz) if hasattr(load, "prepare") else None
        s0 = s1 = s2 = None
        for ix in range(0, NV1, BLOCK):
            read = jnp.concatenate(streamed(load(j + ix, ix, rest), ix, cy, cz), axis=2)
            store(j + ix, read)
            for b in range(BLOCK):
                cx = -speed_limit + spacing * (ix + b)
                one = read[b]
                m1 = cx * one
                m2 = cx * m1
                s0 = one if s0 is None else s0 + one
                s1 = m1 if s1 is None else s1 + m1
                s2 = m2 if s2 is None else s2 + m2
        return (
            sums[0] + s0,
            sums[1] + s1,
            sums[2] + cy * s0,
            sums[3] + cz * s0,
            sums[4] + (s2 + (cy * cy + cz * cz) * s0),
        )

    def chunk(c, load, store, sums):
        def body(i, carry):
            return velocity_row(c * size + i * NV1, load, store, carry)

        return lax.fori_loop(0, size // NV1, body, sums)

    zero = tuple(jnp.zeros((nx, cells), jnp.float32) for _ in range(MOMENTS))
    owner = [(i * nv) // MOMENTS for i in range(MOMENTS)]
    is_owner = functools.reduce(jnp.logical_or, [v == o for o in owner])

    def write_part(which, sums):
        for i in range(MOMENTS):
            for s in range(ng):
                part[which, i, s] = weight * sums[i][s * xs : (s + 1) * xs]

    def scatter(which):
        for i, o in enumerate(owner):
            def over(s, i=i, o=o):
                @pl.when(jnp.logical_not(jnp.logical_and(v == o, g == s)))
                def _():
                    slot = lax.rem(me - (o * ng + s) - 1 + ranks, ranks)
                    pltpu.make_async_remote_copy(
                        src_ref=part.at[which, i, s],
                        dst_ref=inbox.at[which, slot],
                        send_sem=rs_send.at[which],
                        recv_sem=rs_recv.at[which],
                        device_id=(o, s),
                        device_id_type=MESH,
                    ).start()

            loop(ng, over)

    def local(ref, sem):
        return pltpu.make_async_copy(ref, ref, sem)

    def gather(which, everyone):
        peers = ranks if everyone else nv
        for i, o in enumerate(owner):
            @pl.when(v == o)
            def _(i=i):
                local(inbox.at[which], rs_recv.at[which]).wait()

                def add(k, acc):
                    return acc + inbox[which, k]

                acc = lax.fori_loop(0, ranks - 1, add, part[which, i, g])
                total[which, i * ng + g] = acc

                def send(k):
                    if everyone:
                        other = lax.rem(me + k + 1, ranks)
                        target = (other // ng, lax.rem(other, ng))
                    else:
                        target = (lax.rem(v + k + 1, nv), g)
                    pltpu.make_async_remote_copy(
                        src_ref=total.at[which, i * ng + g],
                        dst_ref=total.at[which, i * ng + g],
                        send_sem=ag_send.at[which],
                        recv_sem=ag_recv.at[which],
                        device_id=target,
                        device_id_type=MESH,
                    ).start()

                loop(peers - 1, send)

        items = MOMENTS * ng if everyone else MOMENTS

        @pl.when(is_owner)
        def _():
            local(total.at[which, pl.ds(0, items - 1)], ag_recv.at[which]).wait()

        @pl.when(jnp.logical_not(is_owner))
        def _():
            local(total.at[which, pl.ds(0, items)], ag_recv.at[which]).wait()

    def drain(which, everyone):
        peers = ranks if everyone else nv

        items = MOMENTS * ng

        @pl.when(is_owner)
        def _():
            local(total.at[which, pl.ds(0, items - 1)], rs_send.at[which]).wait()
            local(inbox.at[which, pl.ds(0, peers - 1)], ag_send.at[which]).wait()

        @pl.when(jnp.logical_not(is_owner))
        def _():
            local(total.at[which], rs_send.at[which]).wait()

    def load_first(j, ix, rest):
        return jnp.concatenate([slab[s, pl.ds(j, BLOCK)] for s in range(ng)], axis=1)

    def store_first(j, read):
        field[pl.ds(j, BLOCK)] = read

    def first_chunk(c, sums):
        for d in range(1, ng):
            incoming(d, c).wait_recv()
        return chunk(c, load_first, store_first, sums)

    sums = lax.fori_loop(0, nc, first_chunk, zero)
    write_part(0, sums)
    scatter(0)
    each(incoming, lambda copy: copy.wait_send())
    gather(0, True)
    fill_tables(
        [jnp.concatenate([total[0, i * ng + s] for s in range(ng)], axis=0) for i in range(MOMENTS)],
        table,
        factor,
    )

    def load_second(j, ix, rest):
        return factor[0] * field[pl.ds(j, BLOCK)] + rest * table[0, ix : ix + BLOCK]

    load_second.prepare = lambda iy, iz: factor[1] * table[1, iy] * table[2, iz]

    def store_second(j, read):
        for s in range(ng):
            slab[s, pl.ds(j, BLOCK)] = read[:, s * xs : (s + 1) * xs]

    early = nc // 2

    def second_chunk(c, sums):
        return chunk(c, load_second, store_second, sums)

    def second_sent(c, sums):
        sums = second_chunk(c, sums)
        for d in range(1, ng):
            outgoing(d, c).start()
        return sums

    sums = lax.fori_loop(0, early, second_sent, zero)
    sums = lax.fori_loop(early, nc, second_chunk, sums)
    write_part(1, sums)
    scatter(1)
    each(outgoing, lambda copy: copy.start(), early, nc)
    drain(0, True)
    gather(1, False)
    fill_tables([total[1, i * ng + g] for i in range(MOMENTS)], table2, factor2)

    def relax(source, s, c):
        def body(i):
            j = c * size + i * NV1
            _, iy, iz = parts_of(v * count + s * n + j)
            rest = factor2[1] * table2[1, iy] * table2[2, iz]
            for ix in range(0, NV1, BLOCK):
                out[pl.ds(s * n + j + ix, BLOCK)] = (
                    factor2[0] * source[s, pl.ds(j + ix, BLOCK)] + rest * table2[0, ix : ix + BLOCK]
                )

        loop(size // NV1, body)

    loop(nc, lambda c: relax(slab, g, c))

    def last(c):
        for d in range(1, ng):
            outgoing(d, c).wait_recv()
            relax(back, lax.rem(g - d + ng, ng), c)

    loop(nc, last)
    each(outgoing, lambda copy: copy.wait_send())
    drain(1, False)


def on_device(distribution):
    nv, ng = lax.axis_size("vel"), lax.axis_size("gx")
    count, xs, cells = distribution.shape
    n = count // ng
    nx = xs * ng
    size = max(NV1, n // 8)
    nc = n // size
    f32 = jnp.float32
    dma = pltpu.SemaphoreType.DMA
    return pl.pallas_call(
        functools.partial(kernel, nv, ng),
        out_shape=pltpu.VMEM(distribution.shape, f32),
        in_specs=[pl.BlockSpec(memory_space=pl.ANY)],
        out_specs=pl.BlockSpec(memory_space=pltpu.VMEM),
        scratch_shapes=[
            pltpu.VMEM((ng, n, xs, cells), f32),
            pltpu.VMEM((n, nx, cells), f32),
            pltpu.VMEM((ng, n, xs, cells), f32),
            pltpu.VMEM((COLLISIONS, MOMENTS, ng, xs, cells), f32),
            pltpu.VMEM((COLLISIONS, nv * ng - 1, xs, cells), f32),
            pltpu.VMEM((COLLISIONS, MOMENTS * ng, xs, cells), f32),
            pltpu.VMEM((3, NV1, nx, cells), f32),
            pltpu.VMEM((2, nx, cells), f32),
            pltpu.VMEM((3, NV1, xs, cells), f32),
            pltpu.VMEM((2, xs, cells), f32),
            dma(()),
            dma((max(ng - 1, 1), nc)),
            dma((max(ng - 1, 1), nc)),
            dma((max(ng - 1, 1), nc)),
            dma((max(ng - 1, 1), nc)),
            dma((COLLISIONS,)),
            dma((COLLISIONS,)),
            dma((COLLISIONS,)),
            dma((COLLISIONS,)),
        ],
        compiler_params=pltpu.CompilerParams(collective_id=0, has_side_effects=True),
    )(distribution)


def solution(mesh):
    return jax.shard_map(
        on_device,
        mesh=mesh,
        in_specs=(P("vel", "gx", None),),
        out_specs=P("vel", "gx", None),
        check_vma=False,
    )
```

```python
import functools
import math

import jax
import jax.numpy as jnp
from jax import lax
from jax.experimental import pallas as pl
from jax.experimental.pallas import tpu as pltpu
from jax.sharding import PartitionSpec as P

NV1 = 16
NZ = 16
COLLISIONS = 2
MOMENTS = 5
BLOCK = 16
MESH = pl.DeviceIdType.MESH

speed_limit = 4.0
time_step = 0.05
knudsen = 0.0125
spacing = 2.0 * speed_limit / (NV1 - 1)
weight = spacing**3 / (2.0 * math.pi) ** 1.5


def loop(count, body):
    def wrapped(i, carry):
        body(i)
        return carry

    lax.fori_loop(0, count, wrapped, 0)


def far_first(size, body):
    if size > 64:
        loop(size - 1, lambda k: body(k + 1))
        return
    for gap in sorted(range(1, size), key=lambda gap: -min(gap, size - gap)):
        body(gap)


def component(index):
    return -speed_limit + spacing * index.astype(jnp.float32)


def fill_shifts(shifts):
    cells = shifts.shape[1]
    source = lax.broadcasted_iota(jnp.int32, (cells, cells), 0)
    target = lax.broadcasted_iota(jnp.int32, (cells, cells), 1)
    same = source // NZ == target // NZ
    for way in (0, 1):
        gap = target - source if way else source - target
        along_y = lax.rem(gap + cells, cells)
        along_z = lax.rem(gap + cells, NZ)
        for d, (one, two) in enumerate(
            (
                (along_y == NZ, along_y == 2 * NZ),
                (same & (along_z == 1), same & (along_z == 2)),
            )
        ):
            value = jnp.where(one, 4.0, jnp.where(two, -1.0, 0.0))
            shifts[2 * d + way] = value.astype(jnp.bfloat16)


def streamed(field, ix0, cy, cz, shifts):
    rows, nx, cells = field.shape
    shape = (rows, nx, cells)
    half = 0.5 * time_step
    speeds = [abs(-speed_limit + spacing * (ix0 + b)) for b in range(rows)]
    signs = [ix0 + b >= NV1 // 2 for b in range(rows)]
    low = signs.count(False)
    ay, az = jnp.abs(cy), jnp.abs(cz)
    along_y = shifts[(cy > 0).astype(jnp.int32)]
    along_z = shifts[2 + (cz > 0).astype(jnp.int32)]

    def moved(g, k):
        below = [pltpu.roll(g[:low], nx - k, 1)] if low else []
        above = [pltpu.roll(g[low:], k, 1)] if low < rows else []
        return jnp.concatenate(below + above, axis=0)

    def advanced(g, factor):
        scale = factor * half
        ky, kz = scale * ay, scale * az
        kx = [scale * speed for speed in speeds]
        centre = [3.0 * (k + (ky + kz)) for k in kx]
        spread = lambda values: jnp.stack([jnp.full(shape[1:], k, jnp.float32) for k in values])
        kx, centre = spread(kx), spread(centre)
        flat = g.reshape(rows * nx, cells)
        top = flat.astype(jnp.bfloat16)
        rest = (flat - top.astype(jnp.float32)).astype(jnp.bfloat16)
        both = jnp.concatenate([top, rest], axis=0)

        def apply(matrix):
            d = jnp.dot(both, matrix, preferred_element_type=jnp.float32)
            return (d[: rows * nx] + d[rows * nx :]).reshape(shape)

        dx = 4.0 * moved(g, 1) - moved(g, 2)
        return (field - centre * g) + kx * dx + ky * apply(along_y) + kz * apply(along_z)

    value = advanced(field, 1.0 / 3.0)
    value = advanced(value, 0.5)
    return advanced(value, 1.0)


def fill_tables(moments, table, factor):
    rho = moments[0]
    ux, uy, uz = moments[1] / rho, moments[2] / rho, moments[3] / rho
    temp = (moments[4] / rho - (ux * ux + uy * uy + uz * uz)) / 3.0
    inverse = -0.5 / temp
    mass = None
    for d, u in enumerate((ux, uy, uz)):
        total = None
        for i in range(NV1):
            offset = (-speed_limit + spacing * i) - u
            value = jnp.exp(offset * offset * inverse)
            table[d, i] = value
            total = value if total is None else total + value
        mass = total if mass is None else mass * total
    nu = time_step * rho * jnp.sqrt(temp) / knudsen
    keep = 1.0 / (1.0 + nu)
    factor[0] = keep
    factor[1] = keep * nu * (rho / (weight * mass))


def kernel(
    nv, ng, src, out, slab, field, back, part, inbox, total, table, factor, table2, factor2, shifts,
    own_sem, in_send, in_recv, out_send, out_recv, rs_send, rs_recv, ag_send, ag_recv,
):
    count, xs, cells = src.shape
    n = count // ng
    nx = ng * xs
    nc = in_send.shape[1]
    size = n // nc
    ranks = nv * ng
    v, g = lax.axis_index("vel"), lax.axis_index("gx")
    me = v * ng + g

    barrier = pltpu.get_barrier_semaphore()

    def greet(gap):
        other = lax.rem(me + gap, ranks)
        pl.semaphore_signal(barrier, 1, device_id=(other // ng, lax.rem(other, ng)), device_id_type=MESH)

    far_first(ranks, greet)
    own = pltpu.make_async_copy(src.at[pl.ds(g * n, n)], slab.at[g], own_sem)
    own.start()
    fill_shifts(shifts)
    pl.semaphore_wait(barrier, ranks - 1)

    def incoming(d, c):
        to = lax.rem(g + d, ng)
        return pltpu.make_async_remote_copy(
            src_ref=src.at[pl.ds(to * n + c * size, size)],
            dst_ref=slab.at[g, pl.ds(c * size, size)],
            send_sem=in_send.at[d - 1, c],
            recv_sem=in_recv.at[d - 1, c],
            device_id=(v, to),
            device_id_type=MESH,
        )

    def outgoing(d, c):
        to = lax.rem(g + d, ng)
        return pltpu.make_async_remote_copy(
            src_ref=slab.at[to, pl.ds(c * size, size)],
            dst_ref=back.at[g, pl.ds(c * size, size)],
            send_sem=out_send.at[d - 1, c],
            recv_sem=out_recv.at[d - 1, c],
            device_id=(v, to),
            device_id_type=MESH,
        )

    def each(make, act, first=0, last=nc):
        def over(c):
            for d in range(1, ng):
                act(make(d, c + first))

        loop(last - first, over)

    each(incoming, lambda copy: copy.start())
    own.wait()

    def parts_of(k):
        ix = lax.rem(k, NV1)
        iz = lax.rem(k // NV1, NV1)
        iy = k // (NV1 * NV1)
        return ix, iy, iz

    def velocity_row(j, load, store, sums):
        _, iy, iz = parts_of(v * count + g * n + j)
        cy, cz = component(iy), component(iz)
        rest = load.prepare(iy, iz) if hasattr(load, "prepare") else None
        s0 = s1 = s2 = None
        for ix in range(0, NV1, BLOCK):
            read = streamed(load(j + ix, ix, rest), ix, cy, cz, shifts)
            store(j + ix, read)
            for b in range(BLOCK):
                cx = -speed_limit + spacing * (ix + b)
                one = read[b]
                m1 = cx * one
                m2 = cx * m1
                s0 = one if s0 is None else s0 + one
                s1 = m1 if s1 is None else s1 + m1
                s2 = m2 if s2 is None else s2 + m2
        return (
            sums[0] + s0,
            sums[1] + s1,
            sums[2] + cy * s0,
            sums[3] + cz * s0,
            sums[4] + (s2 + (cy * cy + cz * cz) * s0),
        )

    def chunk(c, load, store, sums):
        def body(i, carry):
            return velocity_row(c * size + i * NV1, load, store, carry)

        return lax.fori_loop(0, size // NV1, body, sums)

    zero = tuple(jnp.zeros((nx, cells), jnp.float32) for _ in range(MOMENTS))
    owner = [(i * nv) // MOMENTS for i in range(MOMENTS)]
    is_owner = functools.reduce(jnp.logical_or, [v == o for o in owner])

    def write_part(which, sums):
        for i in range(MOMENTS):
            for s in range(ng):
                part[which, i, s] = weight * sums[i][s * xs : (s + 1) * xs]

    def scatter(which):
        for i, o in enumerate(owner):
            def over(s, i=i, o=o):
                @pl.when(jnp.logical_not(jnp.logical_and(v == o, g == s)))
                def _():
                    slot = lax.rem(me - (o * ng + s) - 1 + ranks, ranks)
                    pltpu.make_async_remote_copy(
                        src_ref=part.at[which, i, s],
                        dst_ref=inbox.at[which, slot],
                        send_sem=rs_send.at[which],
                        recv_sem=rs_recv.at[which],
                        device_id=(o, s),
                        device_id_type=MESH,
                    ).start()

            loop(ng, over)

    def local(ref, sem):
        return pltpu.make_async_copy(ref, ref, sem)

    def gather(which, everyone):
        peers = ranks if everyone else nv

        @pl.when(is_owner)
        def _():
            i = functools.reduce(jnp.add, [(v > o).astype(jnp.int32) for o in owner])
            local(inbox.at[which], rs_recv.at[which]).wait()
            lanes = [part[which, i, g]] + [jnp.zeros((xs, cells), jnp.float32)] * 3
            if ranks <= 64:
                for k in range(ranks - 1):
                    lanes[k % 4] = lanes[k % 4] + inbox[which, k]
                acc = (lanes[0] + lanes[1]) + (lanes[2] + lanes[3])
            else:
                acc = lax.fori_loop(0, ranks - 1, lambda k, acc: acc + inbox[which, k], lanes[0])
            total[which, i * ng + g] = acc

            def send(gap):
                if everyone:
                    other = lax.rem(me + gap, ranks)
                    target = (other // ng, lax.rem(other, ng))
                else:
                    target = (lax.rem(v + gap, nv), g)
                pltpu.make_async_remote_copy(
                    src_ref=total.at[which, i * ng + g],
                    dst_ref=total.at[which, i * ng + g],
                    send_sem=ag_send.at[which],
                    recv_sem=ag_recv.at[which],
                    device_id=target,
                    device_id_type=MESH,
                ).start()

            far_first(peers, send)

        items = MOMENTS * ng if everyone else MOMENTS

        @pl.when(is_owner)
        def _():
            local(total.at[which, pl.ds(0, items - 1)], ag_recv.at[which]).wait()

        @pl.when(jnp.logical_not(is_owner))
        def _():
            local(total.at[which, pl.ds(0, items)], ag_recv.at[which]).wait()

    def drain(which, everyone):
        peers = ranks if everyone else nv

        items = MOMENTS * ng

        @pl.when(is_owner)
        def _():
            local(total.at[which, pl.ds(0, items - 1)], rs_send.at[which]).wait()
            local(inbox.at[which, pl.ds(0, peers - 1)], ag_send.at[which]).wait()

        @pl.when(jnp.logical_not(is_owner))
        def _():
            local(total.at[which], rs_send.at[which]).wait()

    def load_first(j, ix, rest):
        return jnp.concatenate([slab[s, pl.ds(j, BLOCK)] for s in range(ng)], axis=1)

    def store_first(j, read):
        field[pl.ds(j, BLOCK)] = read

    def first_chunk(c, sums):
        for d in range(1, ng):
            incoming(d, c).wait_recv()
        return chunk(c, load_first, store_first, sums)

    sums = lax.fori_loop(0, nc, first_chunk, zero)
    write_part(0, sums)
    scatter(0)
    each(incoming, lambda copy: copy.wait_send())
    gather(0, True)
    fill_tables(
        [jnp.concatenate([total[0, i * ng + s] for s in range(ng)], axis=0) for i in range(MOMENTS)],
        table,
        factor,
    )

    def load_second(j, ix, rest):
        return factor[0] * field[pl.ds(j, BLOCK)] + rest * table[0, ix : ix + BLOCK]

    load_second.prepare = lambda iy, iz: factor[1] * table[1, iy] * table[2, iz]

    def store_second(j, read):
        for s in range(ng):
            slab[s, pl.ds(j, BLOCK)] = read[:, s * xs : (s + 1) * xs]

    early = nc // 2

    def second_chunk(c, sums):
        return chunk(c, load_second, store_second, sums)

    def second_sent(c, sums):
        sums = second_chunk(c, sums)
        for d in range(1, ng):
            outgoing(d, c).start()
        return sums

    sums = lax.fori_loop(0, early, second_sent, zero)
    sums = lax.fori_loop(early, nc, second_chunk, sums)
    write_part(1, sums)
    scatter(1)
    each(outgoing, lambda copy: copy.start(), early, nc)
    drain(0, True)
    gather(1, False)
    fill_tables([total[1, i * ng + g] for i in range(MOMENTS)], table2, factor2)

    def relax(source, s, c):
        def body(i):
            j = c * size + i * NV1
            _, iy, iz = parts_of(v * count + s * n + j)
            rest = factor2[1] * table2[1, iy] * table2[2, iz]
            for ix in range(0, NV1, BLOCK):
                out[pl.ds(s * n + j + ix, BLOCK)] = (
                    factor2[0] * source[s, pl.ds(j + ix, BLOCK)] + rest * table2[0, ix : ix + BLOCK]
                )

        loop(size // NV1, body)

    loop(nc, lambda c: relax(slab, g, c))

    def last(c):
        for d in range(1, ng):
            outgoing(d, c).wait_recv()
            relax(back, lax.rem(g - d + ng, ng), c)

    loop(nc, last)
    each(outgoing, lambda copy: copy.wait_send())
    drain(1, False)


def on_device(distribution):
    nv, ng = lax.axis_size("vel"), lax.axis_size("gx")
    count, xs, cells = distribution.shape
    n = count // ng
    nx = xs * ng
    size = max(NV1, n // 8)
    nc = n // size
    f32 = jnp.float32
    dma = pltpu.SemaphoreType.DMA
    return pl.pallas_call(
        functools.partial(kernel, nv, ng),
        out_shape=pltpu.VMEM(distribution.shape, f32),
        in_specs=[pl.BlockSpec(memory_space=pl.ANY)],
        out_specs=pl.BlockSpec(memory_space=pltpu.VMEM),
        scratch_shapes=[
            pltpu.VMEM((ng, n, xs, cells), f32),
            pltpu.VMEM((n, nx, cells), f32),
            pltpu.VMEM((ng, n, xs, cells), f32),
            pltpu.VMEM((COLLISIONS, MOMENTS, ng, xs, cells), f32),
            pltpu.VMEM((COLLISIONS, nv * ng - 1, xs, cells), f32),
            pltpu.VMEM((COLLISIONS, MOMENTS * ng, xs, cells), f32),
            pltpu.VMEM((3, NV1, nx, cells), f32),
            pltpu.VMEM((2, nx, cells), f32),
            pltpu.VMEM((3, NV1, xs, cells), f32),
            pltpu.VMEM((2, xs, cells), f32),
            pltpu.VMEM((4, cells, cells), jnp.bfloat16),
            dma(()),
            dma((max(ng - 1, 1), nc)),
            dma((max(ng - 1, 1), nc)),
            dma((max(ng - 1, 1), nc)),
            dma((max(ng - 1, 1), nc)),
            dma((COLLISIONS,)),
            dma((COLLISIONS,)),
            dma((COLLISIONS,)),
            dma((COLLISIONS,)),
        ],
        compiler_params=pltpu.CompilerParams(collective_id=0, has_side_effects=True),
    )(distribution)


def solution(mesh):
    return jax.shard_map(
        on_device,
        mesh=mesh,
        in_specs=(P("vel", "gx", None),),
        out_specs=P("vel", "gx", None),
        check_vma=False,
    )
```

```python
import functools
import math

import jax
import jax.numpy as jnp
from jax import lax
from jax.experimental import pallas as pl
from jax.experimental.pallas import tpu as pltpu
from jax.sharding import PartitionSpec as P

NV1 = 16
NZ = 16
COLLISIONS = 2
MOMENTS = 5
BLOCK = 16
MESH = pl.DeviceIdType.MESH

speed_limit = 4.0
time_step = 0.05
knudsen = 0.0125
spacing = 2.0 * speed_limit / (NV1 - 1)
weight = spacing**3 / (2.0 * math.pi) ** 1.5


def loop(count, body):
    def wrapped(i, carry):
        body(i)
        return carry

    lax.fori_loop(0, count, wrapped, 0)


def far_first(size, body):
    if size > 64:
        loop(size - 1, lambda k: body(k + 1))
        return
    for gap in sorted(range(1, size), key=lambda gap: -min(gap, size - gap)):
        body(gap)


def component(index):
    return -speed_limit + spacing * index.astype(jnp.float32)


def fill_shifts(shifts):
    cells = shifts.shape[1]
    source = lax.broadcasted_iota(jnp.int32, (cells, cells), 0)
    target = lax.broadcasted_iota(jnp.int32, (cells, cells), 1)
    same = source // NZ == target // NZ
    for way in (0, 1):
        gap = target - source if way else source - target
        along_y = lax.rem(gap + cells, cells)
        along_z = lax.rem(gap + cells, NZ)
        for d, (one, two) in enumerate(
            (
                (along_y == NZ, along_y == 2 * NZ),
                (same & (along_z == 1), same & (along_z == 2)),
            )
        ):
            value = jnp.where(one, 4.0, jnp.where(two, -1.0, 0.0))
            shifts[2 * d + way] = value.astype(jnp.bfloat16)


def streamed(field, ix0, cy, cz, shifts):
    rows, nx, cells = field.shape
    shape = (rows, nx, cells)
    half = 0.5 * time_step
    speeds = [abs(-speed_limit + spacing * (ix0 + b)) for b in range(rows)]
    signs = [ix0 + b >= NV1 // 2 for b in range(rows)]
    low = signs.count(False)
    ay, az = jnp.abs(cy), jnp.abs(cz)
    along_y = shifts[(cy > 0).astype(jnp.int32)]
    along_z = shifts[2 + (cz > 0).astype(jnp.int32)]

    def moved(g, k):
        below = [pltpu.roll(g[:low], nx - k, 1)] if low else []
        above = [pltpu.roll(g[low:], k, 1)] if low < rows else []
        return jnp.concatenate(below + above, axis=0)

    def advanced(g, factor):
        scale = factor * half
        ky, kz = scale * ay, scale * az
        kx = [scale * speed for speed in speeds]
        centre = [3.0 * (k + (ky + kz)) for k in kx]
        spread = lambda values: jnp.stack([jnp.full(shape[1:], k, jnp.float32) for k in values])
        kx, centre = spread(kx), spread(centre)
        flat = g.reshape(rows * nx, cells)
        top = flat.astype(jnp.bfloat16)
        rest = (flat - top.astype(jnp.float32)).astype(jnp.bfloat16)
        both = jnp.concatenate([top, rest], axis=0)

        def apply(matrix):
            d = jnp.dot(both, matrix, preferred_element_type=jnp.float32)
            return (d[: rows * nx] + d[rows * nx :]).reshape(shape)

        dx = 4.0 * moved(g, 1) - moved(g, 2)
        return (field - centre * g) + kx * dx + ky * apply(along_y) + kz * apply(along_z)

    value = advanced(field, 1.0 / 3.0)
    value = advanced(value, 0.5)
    return advanced(value, 1.0)


def fill_tables(moments, table, factor):
    rho = moments[0]
    ux, uy, uz = moments[1] / rho, moments[2] / rho, moments[3] / rho
    temp = (moments[4] / rho - (ux * ux + uy * uy + uz * uz)) / 3.0
    inverse = -0.5 / temp
    mass = None
    for d, u in enumerate((ux, uy, uz)):
        total = None
        for i in range(NV1):
            offset = (-speed_limit + spacing * i) - u
            value = jnp.exp(offset * offset * inverse)
            table[d, i] = value
            total = value if total is None else total + value
        mass = total if mass is None else mass * total
    nu = time_step * rho * jnp.sqrt(temp) / knudsen
    keep = 1.0 / (1.0 + nu)
    factor[0] = keep
    factor[1] = keep * nu * (rho / (weight * mass))


def kernel(
    nv, ng, src, out, slab, field, back, part, inbox0, total0, inbox1, total1, table, factor, table2, factor2, shifts,
    known, own_sem, in_send, in_recv, out_send, out_recv, rs_send, rs_recv, ag_send, ag_recv,
):
    count, xs, cells = src.shape
    n = count // ng
    nx = ng * xs
    nc = in_send.shape[1]
    size = n // nc
    ranks = nv * ng
    v, g = lax.axis_index("vel"), lax.axis_index("gx")
    me = v * ng + g

    barrier = pltpu.get_barrier_semaphore()

    bits = ranks.bit_length() - 1
    assert ranks == 1 << bits

    def across(bit):
        other = me + (1 << bit) * (1 - 2 * lax.rem(me // (1 << bit), 2))
        return (other // ng, lax.rem(other, ng))

    def rounds(first, last):
        for bit in range(first, last):
            pl.semaphore_signal(known.at[bit], 1, device_id=across(bit), device_id_type=MESH)
            pl.semaphore_wait(known.at[bit], 1)

    for bit in range(bits):
        pl.semaphore_signal(barrier, 1, device_id=across(bit), device_id_type=MESH)
    own = pltpu.make_async_copy(src.at[pl.ds(g * n, n)], slab.at[g], own_sem)
    own.start()
    fill_shifts(shifts)
    pl.semaphore_wait(barrier, bits)
    near = 0 if ng <= 2 else ng.bit_length() - 1
    rounds(0, near)

    def incoming(d, c):
        to = lax.rem(g + d, ng)
        return pltpu.make_async_remote_copy(
            src_ref=src.at[pl.ds(to * n + c * size, size)],
            dst_ref=slab.at[g, pl.ds(c * size, size)],
            send_sem=in_send.at[d - 1, c],
            recv_sem=in_recv.at[d - 1, c],
            device_id=(v, to),
            device_id_type=MESH,
        )

    def outgoing(d, c):
        to = lax.rem(g + d, ng)
        return pltpu.make_async_remote_copy(
            src_ref=slab.at[to, pl.ds(c * size, size)],
            dst_ref=back.at[g, pl.ds(c * size, size)],
            send_sem=out_send.at[d - 1, c],
            recv_sem=out_recv.at[d - 1, c],
            device_id=(v, to),
            device_id_type=MESH,
        )

    def each(make, act, first=0, last=nc):
        def over(c):
            for d in range(1, ng):
                act(make(d, c + first))

        loop(last - first, over)

    each(incoming, lambda copy: copy.start())
    rounds(near, bits)
    own.wait()

    def parts_of(k):
        ix = lax.rem(k, NV1)
        iz = lax.rem(k // NV1, NV1)
        iy = k // (NV1 * NV1)
        return ix, iy, iz

    def velocity_row(j, load, store, sums):
        _, iy, iz = parts_of(v * count + g * n + j)
        cy, cz = component(iy), component(iz)
        rest = load.prepare(iy, iz) if hasattr(load, "prepare") else None
        s0 = s1 = s2 = None
        for ix in range(0, NV1, BLOCK):
            read = streamed(load(j + ix, ix, rest), ix, cy, cz, shifts)
            store(j + ix, read)
            for b in range(BLOCK):
                cx = -speed_limit + spacing * (ix + b)
                one = read[b]
                m1 = cx * one
                m2 = cx * m1
                s0 = one if s0 is None else s0 + one
                s1 = m1 if s1 is None else s1 + m1
                s2 = m2 if s2 is None else s2 + m2
        return (
            sums[0] + s0,
            sums[1] + s1,
            sums[2] + cy * s0,
            sums[3] + cz * s0,
            sums[4] + (s2 + (cy * cy + cz * cz) * s0),
        )

    def chunk(c, load, store, sums):
        def body(i, carry):
            return velocity_row(c * size + i * NV1, load, store, carry)

        return lax.fori_loop(0, size // NV1, body, sums)

    zero = tuple(jnp.zeros((nx, cells), jnp.float32) for _ in range(MOMENTS))
    owner = [(i * nv) // MOMENTS for i in range(MOMENTS)]
    is_owner = functools.reduce(jnp.logical_or, [v == o for o in owner])

    def write_part(which, sums):
        for i in range(MOMENTS):
            for s in range(ng):
                part[which, i, s] = weight * sums[i][s * xs : (s + 1) * xs]

    inboxes, totals = (inbox0, inbox1), (total0, total1)

    def piece(which, i, s):
        return part.at[0, i] if which == 0 else part.at[1, i, s]

    def scatter(which):
        for i, o in enumerate(owner):
            def over(s, i=i, o=o):
                @pl.when(jnp.logical_not(jnp.logical_and(v == o, g == s)))
                def _():
                    slot = lax.rem(me - (o * ng + s) - 1 + ranks, ranks)
                    pltpu.make_async_remote_copy(
                        src_ref=piece(which, i, s),
                        dst_ref=inboxes[which].at[slot],
                        send_sem=rs_send.at[which],
                        recv_sem=rs_recv.at[which],
                        device_id=(o, s),
                        device_id_type=MESH,
                    ).start()

            loop(ng, over)

    def local(ref, sem):
        return pltpu.make_async_copy(ref, ref, sem)

    def gather(which):
        inbox, total = inboxes[which], totals[which]

        @pl.when(is_owner)
        def _():
            i = functools.reduce(jnp.add, [(v > o).astype(jnp.int32) for o in owner])
            local(inbox, rs_recv.at[which]).wait()
            lanes = [piece(which, i, g)[...]]
            lanes += [jnp.zeros(lanes[0].shape, jnp.float32)] * 3
            if ranks <= 64:
                for k in range(ranks - 1):
                    lanes[k % 4] = lanes[k % 4] + inbox[k]
                acc = (lanes[0] + lanes[1]) + (lanes[2] + lanes[3])
            else:
                acc = lax.fori_loop(0, ranks - 1, lambda k, acc: acc + inbox[k], lanes[0])
            total[i] = acc

            def send(gap):
                pltpu.make_async_remote_copy(
                    src_ref=total.at[i],
                    dst_ref=total.at[i],
                    send_sem=ag_send.at[which],
                    recv_sem=ag_recv.at[which],
                    device_id=(lax.rem(v + gap, nv), g),
                    device_id_type=MESH,
                ).start()

            far_first(nv, send)
            local(total.at[pl.ds(0, MOMENTS - 1)], ag_recv.at[which]).wait()

        @pl.when(jnp.logical_not(is_owner))
        def _():
            local(total, ag_recv.at[which]).wait()

    def drain(which):
        inbox = inboxes[which]

        @pl.when(is_owner)
        def _():
            local(inbox.at[pl.ds(0, MOMENTS * ng - 1)], rs_send.at[which]).wait()
            local(inbox.at[pl.ds(0, nv - 1)], ag_send.at[which]).wait()

        @pl.when(jnp.logical_not(is_owner))
        def _():
            local(inbox.at[pl.ds(0, MOMENTS * ng)], rs_send.at[which]).wait()

    def load_first(j, ix, rest):
        return jnp.concatenate([slab[s, pl.ds(j, BLOCK)] for s in range(ng)], axis=1)

    def store_first(j, read):
        field[pl.ds(j, BLOCK)] = read

    def first_chunk(c, sums):
        for d in range(1, ng):
            incoming(d, c).wait_recv()
        return chunk(c, load_first, store_first, sums)

    sums = lax.fori_loop(0, nc, first_chunk, zero)
    write_part(0, sums)
    scatter(0)
    each(incoming, lambda copy: copy.wait_send())
    gather(0)
    fill_tables(
        [jnp.concatenate([total0[i, s] for s in range(ng)], axis=0) for i in range(MOMENTS)],
        table,
        factor,
    )

    def load_second(j, ix, rest):
        return factor[0] * field[pl.ds(j, BLOCK)] + rest * table[0, ix : ix + BLOCK]

    load_second.prepare = lambda iy, iz: factor[1] * table[1, iy] * table[2, iz]

    def store_second(j, read):
        for s in range(ng):
            slab[s, pl.ds(j, BLOCK)] = read[:, s * xs : (s + 1) * xs]

    early = nc // 2

    def second_chunk(c, sums):
        return chunk(c, load_second, store_second, sums)

    def second_sent(c, sums):
        sums = second_chunk(c, sums)
        for d in range(1, ng):
            outgoing(d, c).start()
        return sums

    sums = lax.fori_loop(0, early, second_sent, zero)
    sums = lax.fori_loop(early, nc, second_chunk, sums)
    write_part(1, sums)
    scatter(1)
    each(outgoing, lambda copy: copy.start(), early, nc)
    drain(0)
    gather(1)
    fill_tables([total1[i] for i in range(MOMENTS)], table2, factor2)

    def relax(source, s, c):
        def body(i):
            j = c * size + i * NV1
            _, iy, iz = parts_of(v * count + s * n + j)
            rest = factor2[1] * table2[1, iy] * table2[2, iz]
            for ix in range(0, NV1, BLOCK):
                out[pl.ds(s * n + j + ix, BLOCK)] = (
                    factor2[0] * source[s, pl.ds(j + ix, BLOCK)] + rest * table2[0, ix : ix + BLOCK]
                )

        loop(size // NV1, body)

    loop(nc, lambda c: relax(slab, g, c))

    def last(c):
        for d in range(1, ng):
            outgoing(d, c).wait_recv()
            relax(back, lax.rem(g - d + ng, ng), c)

    loop(nc, last)
    each(outgoing, lambda copy: copy.wait_send())
    drain(1)


def on_device(distribution):
    nv, ng = lax.axis_size("vel"), lax.axis_size("gx")
    count, xs, cells = distribution.shape
    n = count // ng
    nx = xs * ng
    size = max(NV1, n // 8)
    nc = n // size
    f32 = jnp.float32
    dma = pltpu.SemaphoreType.DMA
    return pl.pallas_call(
        functools.partial(kernel, nv, ng),
        out_shape=pltpu.VMEM(distribution.shape, f32),
        in_specs=[pl.BlockSpec(memory_space=pl.ANY)],
        out_specs=pl.BlockSpec(memory_space=pltpu.VMEM),
        scratch_shapes=[
            pltpu.VMEM((ng, n, xs, cells), f32),
            pltpu.VMEM((n, nx, cells), f32),
            pltpu.VMEM((ng, n, xs, cells), f32),
            pltpu.VMEM((COLLISIONS, MOMENTS, ng, xs, cells), f32),
            pltpu.VMEM((nv * ng - 1, ng, xs, cells), f32),
            pltpu.VMEM((MOMENTS, ng, xs, cells), f32),
            pltpu.VMEM((nv * ng - 1, xs, cells), f32),
            pltpu.VMEM((MOMENTS, xs, cells), f32),
            pltpu.VMEM((3, NV1, nx, cells), f32),
            pltpu.VMEM((2, nx, cells), f32),
            pltpu.VMEM((3, NV1, xs, cells), f32),
            pltpu.VMEM((2, xs, cells), f32),
            pltpu.VMEM((4, cells, cells), jnp.bfloat16),
            pltpu.SemaphoreType.REGULAR(((nv * ng).bit_length(),)),
            dma(()),
            dma((max(ng - 1, 1), nc)),
            dma((max(ng - 1, 1), nc)),
            dma((max(ng - 1, 1), nc)),
            dma((max(ng - 1, 1), nc)),
            dma((COLLISIONS,)),
            dma((COLLISIONS,)),
            dma((COLLISIONS,)),
            dma((COLLISIONS,)),
        ],
        compiler_params=pltpu.CompilerParams(collective_id=0, has_side_effects=True),
    )(distribution)


def solution(mesh):
    return jax.shard_map(
        on_device,
        mesh=mesh,
        in_specs=(P("vel", "gx", None),),
        out_specs=P("vel", "gx", None),
        check_vma=False,
    )
```

```python
import functools
import math

import jax
import jax.numpy as jnp
from jax import lax
from jax.experimental import pallas as pl
from jax.experimental.pallas import tpu as pltpu
from jax.sharding import PartitionSpec as P

NV1 = 16
NZ = 16
COLLISIONS = 2
MOMENTS = 5
BLOCK = 16
MESH = pl.DeviceIdType.MESH

speed_limit = 4.0
time_step = 0.05
knudsen = 0.0125
spacing = 2.0 * speed_limit / (NV1 - 1)
weight = spacing**3 / (2.0 * math.pi) ** 1.5


def loop(count, body):
    def wrapped(i, carry):
        body(i)
        return carry

    lax.fori_loop(0, count, wrapped, 0)


def far_first(size, body):
    if size > 64:
        loop(size - 1, lambda k: body(k + 1))
        return
    for gap in sorted(range(1, size), key=lambda gap: -min(gap, size - gap)):
        body(gap)


def component(index):
    return -speed_limit + spacing * index.astype(jnp.float32)


def fill_shifts(shifts):
    cells = shifts.shape[1]
    source = lax.broadcasted_iota(jnp.int32, (cells, cells), 0)
    target = lax.broadcasted_iota(jnp.int32, (cells, cells), 1)
    same = source // NZ == target // NZ
    for way in (0, 1):
        gap = target - source if way else source - target
        along_y = lax.rem(gap + cells, cells)
        along_z = lax.rem(gap + cells, NZ)
        for d, (one, two) in enumerate(
            (
                (along_y == NZ, along_y == 2 * NZ),
                (same & (along_z == 1), same & (along_z == 2)),
            )
        ):
            value = jnp.where(one, 4.0, jnp.where(two, -1.0, 0.0))
            shifts[2 * d + way] = value.astype(jnp.bfloat16)


def streamed(field, ix0, cy, cz, shifts):
    rows, nx, cells = field.shape
    shape = (rows, nx, cells)
    half = 0.5 * time_step
    speeds = [abs(-speed_limit + spacing * (ix0 + b)) for b in range(rows)]
    signs = [ix0 + b >= NV1 // 2 for b in range(rows)]
    low = signs.count(False)
    ay, az = jnp.abs(cy), jnp.abs(cz)
    along_y = shifts[(cy > 0).astype(jnp.int32)]
    along_z = shifts[2 + (cz > 0).astype(jnp.int32)]

    def moved(g, k):
        below = [pltpu.roll(g[:low], nx - k, 1)] if low else []
        above = [pltpu.roll(g[low:], k, 1)] if low < rows else []
        return jnp.concatenate(below + above, axis=0)

    def advanced(g, factor):
        scale = factor * half
        ky, kz = scale * ay, scale * az
        kx = [scale * speed for speed in speeds]
        centre = [3.0 * (k + (ky + kz)) for k in kx]
        spread = lambda values: jnp.stack([jnp.full(shape[1:], k, jnp.float32) for k in values])
        kx, centre = spread(kx), spread(centre)
        flat = g.reshape(rows * nx, cells)
        top = flat.astype(jnp.bfloat16)
        rest = (flat - top.astype(jnp.float32)).astype(jnp.bfloat16)
        both = jnp.concatenate([top, rest], axis=0)

        def apply(matrix):
            d = jnp.dot(both, matrix, preferred_element_type=jnp.float32)
            return (d[: rows * nx] + d[rows * nx :]).reshape(shape)

        dx = 4.0 * moved(g, 1) - moved(g, 2)
        return (field - centre * g) + kx * dx + ky * apply(along_y) + kz * apply(along_z)

    value = advanced(field, 1.0 / 3.0)
    value = advanced(value, 0.5)
    return advanced(value, 1.0)


def fill_tables(moments, table, factor):
    rho = moments[0]
    ux, uy, uz = moments[1] / rho, moments[2] / rho, moments[3] / rho
    temp = (moments[4] / rho - (ux * ux + uy * uy + uz * uz)) / 3.0
    inverse = -0.5 / temp
    mass = None
    for d, u in enumerate((ux, uy, uz)):
        total = None
        for i in range(NV1):
            offset = (-speed_limit + spacing * i) - u
            value = jnp.exp(offset * offset * inverse)
            table[d, i] = value
            total = value if total is None else total + value
        mass = total if mass is None else mass * total
    nu = time_step * rho * jnp.sqrt(temp) / knudsen
    keep = 1.0 / (1.0 + nu)
    factor[0] = keep
    factor[1] = keep * nu * (rho / (weight * mass))


def kernel(
    nv, ng, src, out, slab, field, back, part, inbox0, total0, inbox1, total1, table, factor, table2, factor2, shifts,
    known, own_sem, in_send, in_recv, out_send, out_recv, rs_send, rs_recv, ag_send, ag_recv,
):
    count, xs, cells = src.shape
    n = count // ng
    nx = ng * xs
    nc = in_send.shape[1]
    size = n // nc
    ranks = nv * ng
    v, g = lax.axis_index("vel"), lax.axis_index("gx")
    me = v * ng + g

    barrier = pltpu.get_barrier_semaphore()

    bits = ranks.bit_length() - 1
    assert ranks == 1 << bits

    def across(bit):
        other = me + (1 << bit) * (1 - 2 * lax.rem(me // (1 << bit), 2))
        return (other // ng, lax.rem(other, ng))

    def rounds(first, last):
        for bit in range(first, last):
            pl.semaphore_signal(known.at[bit], 1, device_id=across(bit), device_id_type=MESH)
            pl.semaphore_wait(known.at[bit], 1)

    for bit in range(bits):
        pl.semaphore_signal(barrier, 1, device_id=across(bit), device_id_type=MESH)
    own = pltpu.make_async_copy(src.at[pl.ds(g * n, n)], slab.at[g], own_sem)
    own.start()
    fill_shifts(shifts)
    pl.semaphore_wait(barrier, bits)
    near = 0 if ng <= 2 else ng.bit_length() - 1
    rounds(0, near)

    def incoming(d, c):
        to = lax.rem(g + d, ng)
        return pltpu.make_async_remote_copy(
            src_ref=src.at[pl.ds(to * n + c * size, size)],
            dst_ref=slab.at[g, pl.ds(c * size, size)],
            send_sem=in_send.at[d - 1, c],
            recv_sem=in_recv.at[d - 1, c],
            device_id=(v, to),
            device_id_type=MESH,
        )

    def outgoing(d, c):
        to = lax.rem(g + d, ng)
        return pltpu.make_async_remote_copy(
            src_ref=slab.at[to, pl.ds(c * size, size)],
            dst_ref=back.at[g, pl.ds(c * size, size)],
            send_sem=out_send.at[d - 1, c],
            recv_sem=out_recv.at[d - 1, c],
            device_id=(v, to),
            device_id_type=MESH,
        )

    def each(make, act, first=0, last=nc):
        def over(c):
            for d in range(1, ng):
                act(make(d, c + first))

        loop(last - first, over)

    each(incoming, lambda copy: copy.start())
    rounds(near, bits)
    own.wait()

    def parts_of(k):
        ix = lax.rem(k, NV1)
        iz = lax.rem(k // NV1, NV1)
        iy = k // (NV1 * NV1)
        return ix, iy, iz

    def velocity_row(j, load, store, sums):
        _, iy, iz = parts_of(v * count + g * n + j)
        cy, cz = component(iy), component(iz)
        rest = load.prepare(iy, iz) if hasattr(load, "prepare") else None
        s0 = s1 = s2 = None
        for ix in range(0, NV1, BLOCK):
            read = streamed(load(j + ix, ix, rest), ix, cy, cz, shifts)
            store(j + ix, read)
            for b in range(BLOCK):
                cx = -speed_limit + spacing * (ix + b)
                one = read[b]
                m1 = cx * one
                m2 = cx * m1
                s0 = one if s0 is None else s0 + one
                s1 = m1 if s1 is None else s1 + m1
                s2 = m2 if s2 is None else s2 + m2
        return (
            sums[0] + s0,
            sums[1] + s1,
            sums[2] + cy * s0,
            sums[3] + cz * s0,
            sums[4] + (s2 + (cy * cy + cz * cz) * s0),
        )

    def chunk(c, load, store, sums):
        def body(i, carry):
            return velocity_row(c * size + i * NV1, load, store, carry)

        return lax.fori_loop(0, size // NV1, body, sums)

    zero = tuple(jnp.zeros((nx, cells), jnp.float32) for _ in range(MOMENTS))
    owner = [(i * nv) // MOMENTS for i in range(MOMENTS)]
    is_owner = functools.reduce(jnp.logical_or, [v == o for o in owner])

    def write_part(which, sums):
        for i in range(MOMENTS):
            for s in range(ng):
                part[which, i, s] = weight * sums[i][s * xs : (s + 1) * xs]

    inboxes, totals = (inbox0, inbox1), (total0, total1)

    def piece(which, i, s):
        return part.at[0, i] if which == 0 else part.at[1, i, s]

    def scatter(which):
        for i, o in enumerate(owner):
            def over(s, i=i, o=o):
                @pl.when(jnp.logical_not(jnp.logical_and(v == o, g == s)))
                def _():
                    slot = lax.rem(me - (o * ng + s) - 1 + ranks, ranks)
                    pltpu.make_async_remote_copy(
                        src_ref=piece(which, i, s),
                        dst_ref=inboxes[which].at[slot],
                        send_sem=rs_send.at[which],
                        recv_sem=rs_recv.at[which],
                        device_id=(o, s),
                        device_id_type=MESH,
                    ).start()

            loop(ng, over)

    def local(ref, sem):
        return pltpu.make_async_copy(ref, ref, sem)

    def gather(which):
        inbox, total = inboxes[which], totals[which]

        @pl.when(is_owner)
        def _():
            i = functools.reduce(jnp.add, [(v > o).astype(jnp.int32) for o in owner])
            local(inbox, rs_recv.at[which]).wait()
            lanes = [piece(which, i, g)[...]]
            lanes += [jnp.zeros(lanes[0].shape, jnp.float32)] * 3
            if ranks <= 64:
                for k in range(ranks - 1):
                    lanes[k % 4] = lanes[k % 4] + inbox[k]
                acc = (lanes[0] + lanes[1]) + (lanes[2] + lanes[3])
            else:
                acc = lax.fori_loop(0, ranks - 1, lambda k, acc: acc + inbox[k], lanes[0])
            total[i] = acc

            def send(gap):
                pltpu.make_async_remote_copy(
                    src_ref=total.at[i],
                    dst_ref=total.at[i],
                    send_sem=ag_send.at[which],
                    recv_sem=ag_recv.at[which],
                    device_id=(lax.rem(v + gap, nv), g),
                    device_id_type=MESH,
                ).start()

            far_first(nv, send)
            local(total.at[pl.ds(0, MOMENTS - 1)], ag_recv.at[which]).wait()

        @pl.when(jnp.logical_not(is_owner))
        def _():
            local(total, ag_recv.at[which]).wait()

    def drain(which):
        inbox = inboxes[which]

        @pl.when(is_owner)
        def _():
            local(inbox.at[pl.ds(0, MOMENTS * ng - 1)], rs_send.at[which]).wait()
            local(inbox.at[pl.ds(0, nv - 1)], ag_send.at[which]).wait()

        @pl.when(jnp.logical_not(is_owner))
        def _():
            local(inbox.at[pl.ds(0, MOMENTS * ng)], rs_send.at[which]).wait()

    def load_first(j, ix, rest):
        return jnp.concatenate([slab[s, pl.ds(j, BLOCK)] for s in range(ng)], axis=1)

    def store_first(j, read):
        field[pl.ds(j, BLOCK)] = read

    def first_chunk(c, sums):
        for d in range(1, ng):
            incoming(d, c).wait_recv()
        return chunk(c, load_first, store_first, sums)

    sums = lax.fori_loop(0, nc, first_chunk, zero)
    write_part(0, sums)
    scatter(0)
    gather(0)
    fill_tables(
        [jnp.concatenate([total0[i, s] for s in range(ng)], axis=0) for i in range(MOMENTS)],
        table,
        factor,
    )

    def load_second(j, ix, rest):
        return factor[0] * field[pl.ds(j, BLOCK)] + rest * table[0, ix : ix + BLOCK]

    load_second.prepare = lambda iy, iz: factor[1] * table[1, iy] * table[2, iz]

    def store_second(j, read):
        for s in range(ng):
            slab[s, pl.ds(j, BLOCK)] = read[:, s * xs : (s + 1) * xs]

    early = nc // 2

    def second_chunk(c, sums):
        return chunk(c, load_second, store_second, sums)

    def second_sent(c, sums):
        sums = second_chunk(c, sums)
        for d in range(1, ng):
            outgoing(d, c).start()
        return sums

    sums = lax.fori_loop(0, early, second_sent, zero)
    sums = lax.fori_loop(early, nc, second_chunk, sums)
    write_part(1, sums)
    scatter(1)
    each(outgoing, lambda copy: copy.start(), early, nc)
    each(incoming, lambda copy: copy.wait_send())
    drain(0)
    gather(1)
    fill_tables([total1[i] for i in range(MOMENTS)], table2, factor2)

    group = 4 if nc % 4 == 0 else 1

    def relax(source, s, c):
        for i in range(group * size // NV1):
            j = c * group * size + i * NV1
            _, iy, iz = parts_of(v * count + s * n + j)
            rest = factor2[1] * table2[1, iy] * table2[2, iz]
            for ix in range(0, NV1, BLOCK):
                out[pl.ds(s * n + j + ix, BLOCK)] = (
                    factor2[0] * source[s, pl.ds(j + ix, BLOCK)] + rest * table2[0, ix : ix + BLOCK]
                )

    loop(nc // group, lambda c: relax(slab, g, c))

    def last(c):
        for d in range(1, ng):
            for k in range(group):
                outgoing(d, c * group + k).wait_recv()
            relax(back, lax.rem(g - d + ng, ng), c)

    loop(nc // group, last)
    each(outgoing, lambda copy: copy.wait_send())
    drain(1)


def on_device(distribution):
    nv, ng = lax.axis_size("vel"), lax.axis_size("gx")
    count, xs, cells = distribution.shape
    n = count // ng
    nx = xs * ng
    size = max(NV1, n // 8)
    nc = n // size
    f32 = jnp.float32
    dma = pltpu.SemaphoreType.DMA
    return pl.pallas_call(
        functools.partial(kernel, nv, ng),
        out_shape=pltpu.VMEM(distribution.shape, f32),
        in_specs=[pl.BlockSpec(memory_space=pl.ANY)],
        out_specs=pl.BlockSpec(memory_space=pltpu.VMEM),
        scratch_shapes=[
            pltpu.VMEM((ng, n, xs, cells), f32),
            pltpu.VMEM((n, nx, cells), f32),
            pltpu.VMEM((ng, n, xs, cells), f32),
            pltpu.VMEM((COLLISIONS, MOMENTS, ng, xs, cells), f32),
            pltpu.VMEM((nv * ng - 1, ng, xs, cells), f32),
            pltpu.VMEM((MOMENTS, ng, xs, cells), f32),
            pltpu.VMEM((nv * ng - 1, xs, cells), f32),
            pltpu.VMEM((MOMENTS, xs, cells), f32),
            pltpu.VMEM((3, NV1, nx, cells), f32),
            pltpu.VMEM((2, nx, cells), f32),
            pltpu.VMEM((3, NV1, xs, cells), f32),
            pltpu.VMEM((2, xs, cells), f32),
            pltpu.VMEM((4, cells, cells), jnp.bfloat16),
            pltpu.SemaphoreType.REGULAR(((nv * ng).bit_length(),)),
            dma(()),
            dma((max(ng - 1, 1), nc)),
            dma((max(ng - 1, 1), nc)),
            dma((max(ng - 1, 1), nc)),
            dma((max(ng - 1, 1), nc)),
            dma((COLLISIONS,)),
            dma((COLLISIONS,)),
            dma((COLLISIONS,)),
            dma((COLLISIONS,)),
        ],
        compiler_params=pltpu.CompilerParams(collective_id=0, has_side_effects=True),
    )(distribution)


def solution(mesh):
    return jax.shard_map(
        on_device,
        mesh=mesh,
        in_specs=(P("vel", "gx", None),),
        out_specs=P("vel", "gx", None),
        check_vma=False,
    )
```
